32 devices in a mesh: row: 4 (over y, core), col: 8 (over z, x).
Axes of the slice: x: 2, y: 2, z: 4, core: 2. Of those that a mesh axis runs over, the one named last changes fastest.
Arguments:
- old_vectors: float32 [8192, 4096], P('row', 'col'), may hold values from -6 to 6, as said below
- pole_values: float32 [8192], replicated, may hold values from 0 to 8192, as said below
- live_mask: int32 [8192], replicated, may hold values from 0 to 1, as said below
- position: int32 [8192], replicated, may hold values from 0 to 8191, as said below
- rank_weight: float32 [1], replicated, may hold values from 0.5 to 2
Outputs:
- new_vectors: float32 [8192, 8192], P('row', 'col')
The draws below stay inside these ranges and needn't reach their ends.
Inputs may be any that keep to these rules, and one draw needn't show every extreme that they name: `pole_values`: strictly increasing; consecutive values differ by 0.2 or more. `old_vectors`: the entries of rows 4095 and 4096 have magnitude 0.5 to 1.5. Each merged position appears exactly once. In every aligned group of 16 consecutive columns s of the halves' eigenvectors (s = h * 4096 + m), exactly 12 have live_mask[position[s]] = 1.
All inputs are finite; a program needn't handle non-finite values.
Results may differ from the reference program's by a relative error of at most 0.0003.
Values sent between devices are 32-bit elements; how exact they have to be, the bound alone decides.
No kernel may reach another device: no remote copies, remote signals or barrier semaphores. Data moves between devices by JAX's collectives and lax.ppermute only.
A program may use at most 128 MiB of HBM per device.

```python
import math
import jax
import jax.numpy as jnp
from jax import lax

ORDER = 8192
HALF = 4096
BISECT = 40
DEFL_GROUP = 16
LIVE_GROUP = 12


def draw_old_vectors(key, part):
    main_key = jax.random.fold_in(key, 11)
    sign_key = jax.random.fold_in(key, 12)
    magnitude_key = jax.random.fold_in(key, 13)
    entries = jnp.clip(jax.random.normal(main_key, (ORDER, HALF), jnp.float32), -6.0, 6.0)
    sign_part = jnp.where(jax.random.bernoulli(sign_key, 0.5, (2, HALF)), 1.0, -1.0)
    magnitude = jax.random.uniform(magnitude_key, (2, HALF), jnp.float32, 0.5, 1.5)
    boundary = sign_part * magnitude
    row_index = jnp.arange(ORDER)[:, None]
    entries = jnp.where(row_index == HALF - 1, boundary[0][None, :], entries)
    entries = jnp.where(row_index == HALF, boundary[1][None, :], entries)
    return entries.astype(jnp.float32)


def draw_pole_values(key, part):
    jitter_key = jax.random.fold_in(key, 21)
    jitter = jax.random.uniform(jitter_key, (ORDER,), jnp.float32, 0.0, 0.4)
    return jnp.arange(ORDER).astype(jnp.float32) + jitter


def deflation_tables(key):
    base_key = jax.random.fold_in(key, 31)
    position = jax.random.permutation(jax.random.fold_in(base_key, 1), ORDER).astype(jnp.int32)
    group_count = ORDER // DEFL_GROUP
    scores = jax.random.randint(jax.random.fold_in(base_key, 2), (group_count, DEFL_GROUP), 0, 1048576)
    sort_keys = scores * DEFL_GROUP + jnp.arange(DEFL_GROUP, dtype=jnp.int32)[None, :]
    ranks = jnp.argsort(jnp.argsort(sort_keys, axis=1), axis=1)
    column_live = (ranks >= DEFL_GROUP - LIVE_GROUP).astype(jnp.int32).reshape(ORDER)
    live_mask = jnp.zeros((ORDER,), jnp.int32).at[position].set(column_live)
    return (position, live_mask)


def draw_live_mask(key, part):
    return deflation_tables(key)[1]


def draw_position(key, part):
    return deflation_tables(key)[0]


def setup_inputs(seed: int = 0) -> dict:
    arg_keys = jax.random.split(jax.random.key(seed), 6)
    return {
        "old_vectors": draw_old_vectors(jax.random.fold_in(arg_keys[5], 71), 0),
        "pole_values": draw_pole_values(jax.random.fold_in(arg_keys[5], 71), 0),
        "live_mask": draw_live_mask(jax.random.fold_in(arg_keys[5], 71), 0),
        "position": draw_position(jax.random.fold_in(arg_keys[5], 71), 0),
        "rank_weight": jnp.clip(jnp.exp(jax.random.uniform(arg_keys[4], (1,), jnp.float32, math.log(0.5), math.log(2.0))), 0.5, 2.0),
    }


def bracket_lengths(pole_values, live_mask, squares, rank_value):
    order_size = pole_values.shape[0]
    positions = jnp.arange(order_size, dtype=jnp.int32)
    marked = jnp.where(live_mask > 0, positions, order_size).astype(jnp.int32)
    shifted = jnp.concatenate([marked[1:], jnp.full((1,), order_size, jnp.int32)])
    following = lax.cummin(shifted, axis=0, reverse=True)
    weight_sum = rank_value * jnp.sum(squares)
    next_gap = pole_values[jnp.minimum(following, order_size - 1)] - pole_values
    return jnp.where(following < order_size, next_gap, weight_sum)

def bisect_roots(pole_here, bracket_len, pole_values, squares, live_mask, rank_value):
    pole_diff = pole_values[None, :] - pole_here[:, None]
    alive_cols = (live_mask > 0)[None, :]

    def halving(interval, unused):
        low_end, high_end = interval
        middle = 0.5 * (low_end + high_end)
        offset_gap = pole_diff - middle[:, None]
        summands = jnp.where(alive_cols, squares[None, :] / jnp.where(alive_cols, offset_gap, 1.0), 0.0)
        secular = 1.0 + rank_value * lax.optimization_barrier(jnp.sum(summands, axis=1))
        is_below = secular < 0.0
        return ((jnp.where(is_below, middle, low_end), jnp.where(is_below, high_end, middle)), None)
    interval, unused = lax.scan(halving, (jnp.zeros_like(bracket_len), bracket_len), None, length=BISECT)
    return 0.5 * (interval[0] + interval[1])

def log_terms(pole_here, offsets, live_here, own_index, pole_values, live_mask):
    order_size = pole_values.shape[0]
    pole_diff = pole_values[None, :] - pole_here[:, None]
    on_pole = own_index[:, None] == jnp.arange(order_size, dtype=jnp.int32)[None, :]
    quotient = jnp.where(on_pole, offsets[:, None], 1.0 - offsets[:, None] / jnp.where(on_pole, 1.0, pole_diff))
    in_play = (live_here[:, None] > 0) & (live_mask[None, :] > 0)
    logs = jnp.where(in_play, jnp.log(jnp.abs(jnp.where(in_play, quotient, 1.0))), 0.0)
    return lax.optimization_barrier(jnp.sum(logs, axis=0))

def column_norms(pole_here, offsets, live_here, pole_values, live_mask, hat_weights):
    alive_cols = (live_mask > 0)[None, :]
    offset_gap = pole_values[None, :] - pole_here[:, None] - offsets[:, None]
    summands = jnp.where(alive_cols, hat_weights[None, :] ** 2 / jnp.where(alive_cols, offset_gap, 1.0) ** 2, 0.0)
    return jnp.where(live_here > 0, jnp.sqrt(lax.optimization_barrier(jnp.sum(summands, axis=1))), 1.0)

def cauchy_tile(sorted_rows, pole_cols, offset_cols, norm_cols, live_cols, col_index, pole_values, live_mask, hat_weights):
    row_poles = pole_values[sorted_rows]
    row_hats = hat_weights[sorted_rows]
    row_live = live_mask[sorted_rows] > 0
    col_live = (live_cols > 0)[None, :]
    both_live = row_live[:, None] & col_live
    offset_gap = row_poles[:, None] - pole_cols[None, :] - offset_cols[None, :]
    entries = row_hats[:, None] / jnp.where(both_live, offset_gap, 1.0) / norm_cols[None, :]
    identity = (sorted_rows[:, None] == col_index[None, :]).astype(jnp.float32)
    return jnp.where(col_live, jnp.where(both_live, entries, 0.0), identity)

def reference(old_vectors, pole_values, live_mask, position, rank_weight):
    rank_value = rank_weight[0]
    boundary = jnp.concatenate([old_vectors[HALF - 1], old_vectors[HALF]])
    spread = jnp.zeros((ORDER,), old_vectors.dtype).at[position].set(boundary)
    coupling = jnp.where(live_mask > 0, spread, 0.0)
    squares = coupling * coupling
    bracket_len = bracket_lengths(pole_values, live_mask, squares, rank_value)
    groups = ORDER // 512
    index_all = jnp.arange(ORDER, dtype=jnp.int32)
    grouped = (pole_values.reshape(groups, 512), bracket_len.reshape(groups, 512), live_mask.reshape(groups, 512), index_all.reshape(groups, 512))

    def solve_group(members):
        bisected = bisect_roots(members[0], members[1], pole_values, squares, live_mask, rank_value)
        return jnp.where(members[2] > 0, bisected, 0.5 * members[1])
    offsets = lax.map(solve_group, grouped).reshape(ORDER)
    offset_groups = offsets.reshape(groups, 512)

    def log_group(members):
        return log_terms(members[0], members[1], members[2], members[3], pole_values, live_mask)
    log_sum = lax.optimization_barrier(jnp.sum(lax.map(log_group, (grouped[0], offset_groups, grouped[2], grouped[3])), axis=0))
    hat_weights = jnp.where(live_mask > 0, jnp.sign(coupling) * jnp.exp(0.5 * (log_sum - jnp.log(rank_value))), 0.0)

    def norm_group(members):
        return column_norms(members[0], members[1], members[2], pole_values, live_mask, hat_weights)
    norms = lax.map(norm_group, (grouped[0], offset_groups, grouped[2])).reshape(ORDER)

    def column_group(members):
        cauchy = cauchy_tile(position, members[0], members[1], members[2], members[3], members[4], pole_values, live_mask, hat_weights)
        top_rows = jnp.dot(old_vectors[:HALF], cauchy[:HALF], precision=lax.Precision.HIGHEST, preferred_element_type=jnp.float32)
        bottom_rows = jnp.dot(old_vectors[HALF:], cauchy[HALF:], precision=lax.Precision.HIGHEST, preferred_element_type=jnp.float32)
        return jnp.concatenate([top_rows, bottom_rows])
    stacked = lax.map(column_group, (grouped[0], offset_groups, norms.reshape(groups, 512), grouped[2], grouped[3]))
    return jnp.transpose(stacked, (1, 0, 2)).reshape(ORDER, ORDER)
```

```python
import functools

import jax
import jax.numpy as jnp
from jax import lax
from jax.experimental import pallas as pl
from jax.experimental.pallas import tpu as pltpu
from jax.sharding import PartitionSpec as P


FAR = 1e30
FIRST = (4, 5, 6)
LANES = 128
F32 = jnp.float32
BF16 = jnp.bfloat16
VMEM = pltpu.VMEM


def whole(shape):
    return pl.BlockSpec(shape, lambda *_: (0,) * len(shape))


def lookup_kernel(slot_ref, table_ref, mask_ref, pole_ref, live_ref):
    count = slot_ref.shape[1]
    width = min(1024, count)
    table = table_ref[...]
    top = table.astype(BF16)
    rest = table - top.astype(F32)
    middle = rest.astype(BF16)
    low = (rest - middle.astype(F32)).astype(BF16)
    stacked = jnp.concatenate([top, middle, low, mask_ref[...].astype(BF16)], axis=0)
    rows = table.shape[1]
    for first in range(0, count, width):
        slot = slot_ref[:, first : first + width]
        chosen = lax.broadcasted_iota(jnp.int32, (rows, width), 0) == (slot >> 7)
        picked = jnp.dot(
            stacked, jnp.where(chosen, 1.0, 0.0).astype(BF16), preferred_element_type=F32
        )
        on_lane = lax.broadcasted_iota(jnp.int32, (LANES, width), 0) == (slot & (LANES - 1))
        value = (picked[:LANES] + picked[LANES : 2 * LANES]) + picked[2 * LANES : 3 * LANES]
        pole_ref[:, first : first + width] = jnp.sum(
            jnp.where(on_lane, value, 0.0), axis=0, keepdims=True
        )
        live_ref[:, first : first + width] = jnp.sum(
            jnp.where(on_lane, picked[3 * LANES :], 0.0), axis=0, keepdims=True
        )


def root_kernel(
    rank_ref, pole_ref, live_ref, edge_ref, own_ref, own_live_ref, root_ref, square, far, delta
):
    alive = live_ref[...] > 0.5
    square[...] = jnp.where(alive, edge_ref[...] * edge_ref[...], 0.0) * rank_ref[0]
    far[...] = jnp.where(alive, pole_ref[...], FAR)
    total = jnp.sum(square[...], axis=1, keepdims=True)
    count = own_ref.shape[0]
    tile = delta.shape[0]
    span = delta.shape[1]
    unroll = 8
    steps = span // (LANES * unroll)

    def spread(column):
        return jnp.broadcast_to(column, (tile, LANES))

    def one_tile(number, carry):
        rows = pl.ds(pl.multiple_of(number * tile, tile), tile)
        here = spread(own_ref[rows, :])

        def prepare(step, sums):
            gap, weight = sums
            for part in range(unroll):
                lanes = pl.ds(pl.multiple_of((step * unroll + part) * LANES, LANES), LANES)
                apart = far[:, lanes] - here
                gap = jnp.minimum(gap, jnp.where(apart > 0.0, apart, FAR))
                at_own = apart == 0.0
                weight = weight + jnp.where(at_own, square[:, lanes], 0.0)
                delta[:, lanes] = jnp.where(at_own, FAR, apart)
            return gap, weight

        zero = jnp.zeros((tile, LANES), F32)
        gap, weight = lax.fori_loop(0, steps, prepare, (zero + FAR, zero))
        gap = jnp.min(gap, axis=1, keepdims=True)
        weight = jnp.sum(weight, axis=1, keepdims=True)
        is_last = gap > 0.1 * FAR
        length = jnp.where(is_last, jnp.broadcast_to(total, gap.shape), gap)
        own_live = own_live_ref[rows, :] > 0

        def improve(state):
            turn, _, low, high, point = state
            shift = spread(point)

            def gather(step, sums):
                value, slope = sums
                for part in range(unroll):
                    lanes = pl.ds(pl.multiple_of((step * unroll + part) * LANES, LANES), LANES)
                    inverse = 1.0 / (delta[:, lanes] - shift)
                    term = square[:, lanes] * inverse
                    value = value + term
                    slope = slope + term * inverse
                return value, slope

            value, slope = lax.fori_loop(0, steps, gather, (zero, zero))
            value = 1.0 + jnp.sum(value, axis=1, keepdims=True)
            slope = jnp.sum(slope, axis=1, keepdims=True)
            is_below = value - weight / point < 0.0
            low = jnp.where(is_below, point, low)
            high = jnp.where(is_below, high, point)
            ahead = length - point
            near = jnp.where(is_last, weight + slope * point * point, weight)
            other = jnp.where(is_last, 0.0, slope * ahead * ahead)
            constant = jnp.where(is_last, value + slope * point, value - slope * ahead)
            middle = constant * length + near + other
            lean = constant * length - near + other
            spread_root = jnp.sqrt(lean * lean + 4.0 * near * other)
            rising = middle > 0.0
            target = jnp.where(
                rising,
                2.0 * near * length / jnp.where(rising, middle + spread_root, 1.0),
                (middle - spread_root) / jnp.where(rising, 1.0, 2.0 * constant),
            )
            change = jnp.abs(target - point)
            fits = ((target >= low) & (target <= high)) | (change <= 1e-5 * point)
            target = jnp.where(fits, target, 0.5 * (low + high))
            change = jnp.abs(target - point)
            still = jnp.where(own_live & (change > 4e-6 * target), 1.0, 0.0)
            return turn + 1, jnp.max(still), low, high, target

        start = 0.5 * length
        state = (jnp.int32(0), jnp.float32(1.0), jnp.zeros_like(length), length, start)
        state = lax.while_loop(lambda s: (s[0] < 48) & (s[1] > 0.5), improve, state)
        root_ref[rows, :] = jnp.where(own_live, state[4], 0.5 * length)
        return carry

    lax.fori_loop(0, count // tile, one_tile, 0)


def log_kernel(pole_ref, column_ref, sum_ref):
    count = pole_ref.shape[1]
    width = min(512, count)
    depth = column_ref.shape[0]
    group = 4
    for first in range(0, count, width):
        here = pole_ref[:, first : first + width]

        def body(step, total):
            product = None
            for part in range(group):
                rows = pl.ds(pl.multiple_of((step * group + part) * 8, 8), 8)
                offset = column_ref[rows, 1:2]
                apart = here - column_ref[rows, 0:1]
                ratio = jnp.where(apart == 0.0, offset, 1.0 - offset / apart)
                product = ratio if product is None else product * ratio
            return total + jnp.log(jnp.abs(product))

        total = lax.fori_loop(
            0, depth // (8 * group), body, jnp.zeros((8, width), F32), unroll=2
        )
        sum_ref[:, first : first + width] = jnp.sum(total, axis=0, keepdims=True)


def norm_kernel(far_ref, hat_ref, column_ref, norm_ref):
    count = column_ref.shape[0]
    span = far_ref.shape[1]
    tile = min(32, count)
    unroll = 8

    def one_tile(number, carry):
        rows = pl.ds(pl.multiple_of(number * tile, tile), tile)
        here = jnp.broadcast_to(column_ref[rows, 0:1], (tile, LANES))
        offset = jnp.broadcast_to(column_ref[rows, 1:2], (tile, LANES))

        def body(step, total):
            for part in range(unroll):
                lanes = pl.ds(pl.multiple_of((step * unroll + part) * LANES, LANES), LANES)
                entry = hat_ref[:, lanes] / ((far_ref[:, lanes] - here) - offset)
                total = total + entry * entry
            return total

        total = lax.fori_loop(0, span // (LANES * unroll), body, jnp.zeros((tile, LANES), F32))
        norm = jnp.sqrt(jnp.sum(total, axis=1, keepdims=True))
        norm_ref[rows, :] = jnp.where(column_ref[rows, 2:3] > 0.5, norm, 1.0)
        return carry

    lax.fori_loop(0, count // tile, one_tile, 0)


def cauchy_kernel(place_ref, column_ref, row_ref, high_ref, low_ref):
    depth, _ = high_ref.shape
    strip = 16
    pole_cols = row_ref[0:1, :]
    offset_cols = row_ref[1:2, :]
    dropped_cols = row_ref[2:3, :]
    live_cols = row_ref[3:4, :]

    def body(step, carry):
        rows = pl.ds(pl.multiple_of(step * strip, strip), strip)
        gap = (column_ref[rows, 0:1] - pole_cols) - offset_cols
        entry = (column_ref[rows, 2:3] / gap) * live_cols
        entry = jnp.where(column_ref[rows, 1:2] == dropped_cols, 1.0, entry)
        high = entry.astype(BF16)
        high_ref[rows, :] = high
        low_ref[rows, :] = (entry - high.astype(F32)).astype(BF16)
        return carry

    lax.fori_loop(0, depth // strip, body, 0, unroll=4)


def product_kernel(pieces, place_ref, *refs):
    piece_refs = refs[:pieces]
    weight_ref, high_ref, low_ref, out_ref, split = refs[pieces:]
    rows, depth = piece_refs[0].shape

    @pl.when(pl.program_id(0) == 0)
    def _():
        for number in range(pieces):
            value = piece_refs[number][...] * weight_ref[pl.ds(place_ref[number], 1), :]
            high = value.astype(BF16)
            lanes = slice(number * depth, (number + 1) * depth)
            split[:rows, lanes] = high
            split[rows:, lanes] = (value - high.astype(F32)).astype(BF16)

    both = jnp.dot(split[...], high_ref[...], preferred_element_type=F32)
    cross = jnp.dot(split[:rows, :], low_ref[...], preferred_element_type=F32)
    out_ref[...] = both[:rows] + (both[rows:] + cross)


def xor_permute(value, bit, count):
    return lax.ppermute(value, "col", [(source, source ^ bit) for source in range(count)])


def xor_gather(value, count, limit, axis):
    rank = lax.axis_index("col")
    bit = 1
    while bit < limit:
        other = xor_permute(value, bit, count)
        after = (rank & bit) > 0
        value = jnp.concatenate(
            [jnp.where(after, other, value), jnp.where(after, value, other)], axis=axis
        )
        bit *= 2
    return value


def shards(old_vectors, pole_values, live_mask, position, rank_weight):
    order_size = pole_values.shape[0]
    half_order = order_size // 2
    rows_here, cols_here = old_vectors.shape
    row_count = lax.axis_size("row")
    col_count = lax.axis_size("col")
    row_rank = lax.axis_index("row")
    col_rank = lax.axis_index("col")
    group = min(4, col_count)
    block_cols = order_size // col_count
    per_device = block_cols // row_count
    quarter = rows_here // group
    cut = quarter // 2
    chunks = ((0, cut), (cut, quarter - cut))
    member = col_rank % group
    half_id = row_rank * rows_here // half_order
    half_base = half_id * half_order

    table_rows = order_size // LANES
    pole_list, live_list = pl.pallas_call(
        lookup_kernel,
        out_shape=[jax.ShapeDtypeStruct((1, order_size), F32)] * 2,
        name="lookup",
    )(
        position[None, :],
        pole_values.reshape(table_rows, LANES).T,
        live_mask.astype(F32).reshape(table_rows, LANES).T,
    )

    upper_owner = (half_order - 1) // rows_here
    lower_owner = half_order // rows_here
    edge = jnp.stack(
        [
            jnp.where(row_rank == upper_owner, old_vectors[(half_order - 1) % rows_here], 0.0),
            jnp.where(row_rank == lower_owner, old_vectors[half_order % rows_here], 0.0),
        ]
    )
    edge = lax.psum(edge, "row")
    edge = xor_gather(edge, col_count, col_count, 1).reshape(1, order_size)

    def send(chunk, bit, token):
        first, count = chunks[chunk]
        target = (member ^ (bit % group)) * quarter + first
        part = lax.dynamic_slice_in_dim(old_vectors, target, count, 0)
        if not bit:
            return part
        if token is not None:
            part, _ = lax.optimization_barrier((part, token))
        return xor_permute(part, bit, col_count)

    pieces = [{}, {}]
    for number, bit in enumerate(FIRST):
        if bit < col_count:
            pieces[0][bit] = send(0, bit, None if number == 0 else edge)

    block_first = col_rank * block_cols
    own_first = block_first + row_rank * per_device
    own_poles = lax.dynamic_slice_in_dim(pole_values, own_first, per_device)[:, None]
    own_live = lax.dynamic_slice_in_dim(live_mask, own_first, per_device)[:, None]
    tile = min(32, per_device)
    in_vmem = pl.BlockSpec(memory_space=VMEM)
    solve = pl.pallas_call(
        root_kernel,
        out_shape=jax.ShapeDtypeStruct((per_device, 1), F32),
        in_specs=[pl.BlockSpec(memory_space=pltpu.SMEM)] + [in_vmem] * 5,
        out_specs=in_vmem,
        scratch_shapes=[
            VMEM((1, order_size), F32),
            VMEM((1, order_size), F32),
            VMEM((tile, order_size), F32),
        ],
        name="roots",
    )
    own_offsets = solve(rank_weight, pole_list, live_list, edge, own_poles, own_live)

    block_offsets = lax.all_gather(own_offsets[:, 0], "row", axis=0, tiled=True)
    block_poles = lax.dynamic_slice_in_dim(pole_values, block_first, block_cols)
    block_live = lax.dynamic_slice_in_dim(live_mask, block_first, block_cols) > 0

    group_offsets = xor_gather(block_offsets[None, :], col_count, group, 1)

    range_cols = order_size // row_count
    range_first = row_rank * range_cols
    range_poles = lax.dynamic_slice_in_dim(pole_list, range_first, range_cols, 1)
    log_sum = pl.pallas_call(
        log_kernel,
        out_shape=jax.ShapeDtypeStruct((1, range_cols), F32),
        name="logs",
    )(
        range_poles,
        jnp.stack([block_poles, jnp.where(block_live, block_offsets, 0.0)], axis=1),
    )
    bit = 1
    while bit < col_count:
        log_sum = log_sum + xor_permute(log_sum, bit, col_count)
        bit *= 2

    def send_rest(chunk, token):
        for bit in list(range(group, col_count)) + list(range(group)):
            if bit not in pieces[chunk]:
                pieces[chunk][bit] = send(chunk, bit, token)

    send_rest(0, (log_sum, group_offsets))
    range_edge = lax.dynamic_slice_in_dim(edge, range_first, range_cols, 1)
    range_live = lax.dynamic_slice_in_dim(live_list, range_first, range_cols, 1) > 0.5
    hats = jnp.where(
        range_live,
        jnp.sign(range_edge) * jnp.exp(0.5 * (log_sum - jnp.log(rank_weight[0]))),
        0.0,
    )
    hats = lax.all_gather(hats, "row", axis=1, tiled=True)
    send_rest(1, hats)
    far_list = jnp.where(live_list > 0.5, pole_list, FAR)

    group_first = (col_rank // group) * group * block_cols
    group_cols = group * block_cols
    group_poles = lax.dynamic_slice_in_dim(pole_values, group_first, group_cols)[None, :]
    group_live = lax.dynamic_slice_in_dim(live_mask, group_first, group_cols)[None, :] > 0
    row_table = jnp.concatenate(
        [
            jnp.where(group_live, group_poles, -FAR),
            group_offsets,
            jnp.where(group_live, -2.0, group_poles),
            group_live.astype(F32),
        ],
        axis=0,
    )
    half_poles = lax.dynamic_slice_in_dim(pole_list[0], half_base, half_order)
    half_live = lax.dynamic_slice_in_dim(live_list[0], half_base, half_order) > 0.5
    column_table = jnp.stack(
        [
            jnp.where(half_live, half_poles, FAR),
            jnp.where(half_live, -1.0, half_poles),
            half_live.astype(F32),
        ],
        axis=1,
    )
    half_hats = lax.dynamic_slice_in_dim(hats[0], half_base, half_order)
    weights = jnp.where(half_live, half_hats, 1.0).reshape(col_count, cols_here)
    row_table, _ = lax.optimization_barrier((row_table, log_sum))
    sources = jnp.bitwise_xor(col_rank, jnp.arange(col_count, dtype=jnp.int32)).astype(jnp.int32)
    wide = min(1024, block_cols)
    tiles = block_cols // wide

    def cauchy(bit):
        place = jnp.concatenate([sources, (member ^ bit)[None].astype(jnp.int32)])
        grid_spec = pltpu.PrefetchScalarGridSpec(
            num_scalar_prefetch=1,
            grid=(col_count, tiles),
            in_specs=[
                pl.BlockSpec((cols_here, 3), lambda i, j, place: (place[i], 0)),
                pl.BlockSpec((4, wide), lambda i, j, place: (0, place[col_count] * tiles + j)),
            ],
            out_specs=[pl.BlockSpec((cols_here, wide), lambda i, j, place: (i, j))] * 2,
        )
        return pl.pallas_call(
            cauchy_kernel,
            out_shape=[jax.ShapeDtypeStruct((half_order, block_cols), BF16)] * 2,
            grid_spec=grid_spec,
            cost_estimate=pl.CostEstimate(
                flops=20 * half_order * block_cols,
                bytes_accessed=4 * half_order * block_cols,
                transcendentals=half_order * block_cols,
            ),
            name="cauchy",
        )(place, column_table, row_table)

    tile_cols = min(256, block_cols)

    def product(parts, high, low):
        rows = parts[0].shape[0]
        grid_spec = pltpu.PrefetchScalarGridSpec(
            num_scalar_prefetch=1,
            grid=(block_cols // tile_cols,),
            in_specs=[whole((rows, cols_here))] * col_count
            + [whole((col_count, cols_here))]
            + [pl.BlockSpec((half_order, tile_cols), lambda i, place: (0, i))] * 2,
            out_specs=pl.BlockSpec((rows, tile_cols), lambda i, place: (0, i)),
            scratch_shapes=[VMEM((2 * rows, half_order), BF16)],
        )
        return pl.pallas_call(
            functools.partial(product_kernel, col_count),
            out_shape=jax.ShapeDtypeStruct((rows, block_cols), F32),
            grid_spec=grid_spec,
            cost_estimate=pl.CostEstimate(
                flops=6 * rows * half_order * block_cols,
                bytes_accessed=4 * half_order * block_cols,
                transcendentals=0,
            ),
            name="product",
        )(sources, *parts, weights, high, low)

    order = list(range(group - 1, -1, -1))
    cauchys = {}
    for bit in order:
        cauchys[bit] = cauchy(bit)
    blocks = []
    for chunk in range(2):
        parts = [pieces[chunk][bit] for bit in range(col_count)]
        done = {}
        for bit in order:
            done[bit] = product(parts, *cauchys[bit])
        for bit in order[-1:] + order[:-1]:
            block = xor_permute(done[bit], bit, col_count) if bit else done[bit]
            blocks.append((block, (member ^ bit) * quarter + chunks[chunk][0]))
    norm_hats, _ = lax.optimization_barrier((hats, done[order[-2]]))
    measure = pl.pallas_call(
        norm_kernel,
        out_shape=jax.ShapeDtypeStruct((per_device, 1), F32),
        name="norms",
    )
    norms = measure(
        far_list,
        norm_hats,
        jnp.concatenate([own_poles, own_offsets, own_live.astype(F32)], axis=1),
    )
    block_norms = lax.all_gather(norms[:, 0], "row", axis=0, tiled=True)[None, :]
    new_vectors = jnp.zeros((rows_here, block_cols), F32)
    for block, first in blocks:
        new_vectors = lax.dynamic_update_slice_in_dim(new_vectors, block / block_norms, first, 0)
    return new_vectors


def solution(mesh):
    in_specs = (P("row", "col"), P(), P(), P(), P())
    out_specs = P("row", "col")
    return jax.shard_map(shards, mesh=mesh, in_specs=in_specs, out_specs=out_specs, check_vma=False)
```
